256 devices in a mesh: band: 32 (over y_lo, z, core), fft: 8 (over y_hi, x).
Axes of the slice: x: 4, y: 4 (y_hi: 2, y_lo: 2; y = y_hi * 2 + y_lo), z: 8, core: 2. Of those that a mesh axis runs over, the one named last changes fastest.
Arguments:
- orbitals: float32 [64, 128, 128, 128], P('band', 'fft'), may hold values from -6 to 6
- owners: int32 [1], replicated, may hold values from 0 to 31
- local_pick: int32 [32, 1], P('band'), may hold values from 0 to 1
Outputs:
- exchange_term: float32 [32, 128, 128, 128], P('band', 'fft')
The draws below stay inside these ranges and needn't reach their ends.
All inputs are finite; a program needn't handle non-finite values.
Results may differ from the reference program's by a relative error of at most 0.0003.
Values sent between devices are 32-bit elements; how exact they have to be, the bound alone decides.
A program may use at most 64 MiB of HBM per device.

```python
import math
import jax
import jax.numpy as jnp
from jax import lax

NG = 128
ORB_DEV = 2
LOC = 1
ROUNDS = 1
BANDS = 64
N_BAND = 32


def plant(values, key, smallest, top_value):
    index_at = [jax.random.randint(jax.random.fold_in(key, axis), (), 0, length) for axis, length in enumerate(values.shape)]
    main_axis = values.shape.index(max(values.shape))
    neighbour = index_at[:main_axis] + [(index_at[main_axis] + 1) % values.shape[main_axis]] + index_at[main_axis + 1:]
    return values.at[tuple(index_at)].set(smallest).at[tuple(neighbour)].set(top_value)


def level_of(own_key, dims, split, low, high):
    def one(dim, shards_of):
        heights = jax.random.uniform(jax.random.fold_in(jax.random.fold_in(own_key, 6), dim), (shards_of,), jnp.float32, low / len(split), high / len(split))
        return jnp.repeat(jnp.exp(heights), dims[dim] // shards_of).reshape((-1,) + (1,) * (len(dims) - dim - 1))

    factor_of = one(*split[0])
    for cut in split[1:]:
        factor_of = factor_of * one(*cut)
    return factor_of


def centred(stream_key, extent, deviation, bound, shards=(), kind=jnp.bfloat16):
    values = deviation * jax.random.normal(stream_key, extent, jnp.float32)
    if shards:
        values = values * level_of(stream_key, extent, shards, -0.22, 0.18)
    return jnp.clip(values, -bound, bound).astype(kind)


def setup_inputs(seed: int = 0) -> dict:
    key_list = jax.random.split(jax.random.key(seed), 4)
    orbitals = centred(key_list[0], (BANDS, NG, NG, NG), 1.0, 6.0, ((0, 32), (1, 8)), jnp.float32)
    owners = jax.random.randint(key_list[1], (ROUNDS,), 0, N_BAND).astype(jnp.int32)
    local_pick = plant(jax.random.randint(key_list[2], (N_BAND, LOC), 0, ORB_DEV), jax.random.fold_in(key_list[2], 1), 0, ORB_DEV - 1).astype(jnp.int32)
    return dict(orbitals=orbitals, owners=owners, local_pick=local_pick)


def signed_freq(size):
    index = jnp.arange(size)
    return jnp.where(index < size // 2, index, index - size).astype(jnp.float32)

def coulomb_table():
    freq = signed_freq(NG)
    square = freq[:, None, None] ** 2 + freq[None, :, None] ** 2 + freq[None, None, :] ** 2
    scale = 0.25 * NG * math.sqrt(NG)
    return jnp.where(square > 0, scale / jnp.maximum(square, 1.0), 0.0)

def reference(orbitals, owners, local_pick):
    coulomb = coulomb_table()
    groups = jnp.arange(N_BAND, dtype=jnp.int32)[:, None]
    picked = (groups * ORB_DEV + local_pick).reshape(-1).astype(jnp.int32)
    sent_all = []
    for step in range(ROUNDS):
        start = (owners[step] * ORB_DEV).astype(jnp.int32)
        sent_all.append(lax.dynamic_slice_in_dim(orbitals, start, ORB_DEV, 0))

    def one_band(index):
        selected = lax.dynamic_index_in_dim(orbitals, index, 0, keepdims=False)
        total = jnp.zeros(selected.shape, jnp.float32)
        for sent in sent_all:
            for orbit in range(ORB_DEV):
                partner = sent[orbit]
                density = partner * selected
                potential = jnp.real(jnp.fft.ifftn(jnp.fft.fftn(density) * coulomb))
                total = total + potential * partner
        return total
    return lax.map(one_band, picked)
```

```python
import functools
import math

import jax
import jax.numpy as jnp
import numpy as np
from jax import lax
from jax.experimental import pallas as pl
from jax.experimental.pallas import tpu as pltpu
from jax.sharding import PartitionSpec as P

NG = 128
NZ = 8
NX = 4
FFT = 8
WIDE = NG // FFT
MESH = pl.DeviceIdType.MESH
SCALE = 0.25 * NG * math.sqrt(NG) / (NG * NG * NG)
ORDER = (1, 3, 4, 2, 5, 7, 6)


def tables():
    index = np.arange(NG)
    angle = (index[:, None] * index[None, :] % NG) * (2.0 * np.pi / NG)
    cosine, sine = np.cos(angle), np.sin(angle)
    right = np.block([[cosine, -sine], [sine, cosine]])
    out = []
    for table in (right, right.T):
        high = table.astype(jnp.bfloat16)
        low = (table - high.astype(np.float64)).astype(jnp.bfloat16)
        out += [high, low]
    return out


def split(value):
    high = value.astype(jnp.bfloat16)
    low = (value - high.astype(jnp.float32)).astype(jnp.bfloat16)
    return high, low


def dot(a, b):
    return jnp.dot(a, b, preferred_element_type=jnp.float32)


def on_right(value, high, low):
    vh, vl = split(value)
    return dot(vh, high) + (dot(vl, high) + dot(vh, low))


def on_left(high, low, value):
    vh, vl = split(value)
    return dot(high, vh) + (dot(high, vl) + dot(low, vh))


def stack(parts):
    return jnp.concatenate([jnp.concatenate(p, axis=0) for p in parts], axis=1)


def unstack(value):
    return jnp.concatenate(
        [
            jnp.concatenate([value[:NG, s], value[NG:, s]], axis=1)
            for s in (slice(0, NG), slice(NG, 2 * NG))
        ],
        axis=0,
    )


CHUNKS = 32
ROWS = WIDE * NG // CHUNKS


def spread_kernel(owner, x_ref, o_ref, ring_recv, pair_recv, ring_send, pair_send, root_send):
    y0, z0, c0 = owner // 16, owner // 2 % NZ, owner % 2
    band = lax.axis_index("band")
    y, z, c = band // 16, lax.rem(band // 2, NZ), lax.rem(band, 2)
    up, down = lax.rem(z + 1, NZ), lax.rem(z + NZ - 1, NZ)

    def at(yy, zz, cc):
        return {"band": yy * 16 + zz * 2 + cc}

    barrier = pltpu.get_barrier_semaphore()
    greet = [at(y, zz, cc) for zz in (up, down) for cc in (0, 1)]
    greet += [at(1 - y, z, cc) for cc in (0, 1)] + [at(y, z, 1 - c)]
    for device in greet:
        pl.semaphore_signal(barrier, inc=1, device_id=device, device_id_type=MESH)
    pl.semaphore_wait(barrier, len(greet))

    ahead = lax.rem(z - z0 + NZ, NZ)
    home = y == y0
    at_root = jnp.logical_and(home, ahead == 0)
    is_owner = jnp.logical_and(at_root, c == c0)
    goes_up = ahead < 4
    goes_down = jnp.logical_or(ahead == 0, ahead > 5)

    def piece(ref, orbital, i):
        return ref.at[orbital, pl.ds(i * ROWS, ROWS)]

    def send(src, orbital, i, send_sem, recv_sem, device):
        return pltpu.make_async_remote_copy(
            piece(src, orbital, i),
            piece(o_ref, orbital, i),
            send_sem,
            recv_sem,
            device_id=device,
            device_id_type=MESH,
        )

    @pl.when(is_owner)
    def _():
        def step(i, carry):
            for j in (0, 1):
                for kind, device in enumerate((at(y0, up, j), at(y0, down, j), at(1 - y0, z, j))):
                    send(x_ref, j, i, root_send.at[kind, j], ring_recv.at[i], device).start()
            return carry

        lax.fori_loop(0, CHUNKS, step, 0)
        whole = pltpu.make_async_remote_copy(
            x_ref, o_ref, pair_send.at[0], pair_recv, device_id=at(y0, z0, 1 - c0), device_id_type=MESH
        )
        whole.start()
        local = pltpu.make_async_copy(x_ref, o_ref, pair_send.at[1])
        local.start()
        for kind in range(3):
            for j in (0, 1):
                pltpu.make_async_copy(x_ref.at[0], x_ref.at[0], root_send.at[kind, j]).wait()
        whole.wait_send()
        local.wait()

    @pl.when(jnp.logical_and(at_root, c != c0))
    def _():
        pltpu.make_async_copy(x_ref, o_ref, pair_recv).wait()

    @pl.when(jnp.logical_not(at_root))
    def _():
        def step(i, carry):
            here = piece(o_ref, c, i)
            pltpu.make_async_copy(here, here, ring_recv.at[i]).wait()

            @pl.when(goes_up)
            def _():
                send(o_ref, c, i, ring_send.at[0], ring_recv.at[i], at(y, up, c)).start()

            @pl.when(goes_down)
            def _():
                send(o_ref, c, i, ring_send.at[1], ring_recv.at[i], at(y, down, c)).start()

            send(o_ref, c, i, pair_send.at[0], pair_recv, at(y, z, 1 - c)).start()
            return carry

        lax.fori_loop(0, CHUNKS, step, 0)
        block = o_ref.at[0]
        pltpu.make_async_copy(block, block, pair_send.at[0]).wait()

        @pl.when(goes_up)
        def _():
            pltpu.make_async_copy(block, block, ring_send.at[0]).wait()

        @pl.when(goes_down)
        def _():
            pltpu.make_async_copy(block, block, ring_send.at[1]).wait()

        pltpu.make_async_copy(block, block, pair_recv).wait()


def spread(owner, orbitals):
    vmem = pl.BlockSpec(memory_space=pltpu.VMEM)
    dma = pltpu.SemaphoreType.DMA
    flat = orbitals.reshape(2, WIDE * NG, NG)
    out = pl.pallas_call(
        functools.partial(spread_kernel, owner),
        out_shape=jax.ShapeDtypeStruct(flat.shape, flat.dtype),
        in_specs=[vmem],
        out_specs=vmem,
        scratch_shapes=[dma((CHUNKS,)), dma, dma((2,)), dma((2,)), dma((3, 2))],
        compiler_params=pltpu.CompilerParams(collective_id=1 + owner, has_side_effects=True),
        name=f"spread_{owner}",
    )(flat)
    return out.reshape(orbitals.shape)


def exchange(send_ref, recv_ref, start, count, send_sem, recv_sem, me):
    high, low = me // NX, lax.rem(me, NX)
    for k in ORDER:
        there = lax.rem(high + k // NX, 2) * NX + lax.rem(low + k % NX, NX)
        pltpu.make_async_remote_copy(
            send_ref.at[pl.ds(start, count), :, pl.ds(there * WIDE, WIDE)],
            recv_ref.at[pl.ds(me * WIDE + start, count)],
            send_sem.at[k],
            recv_sem.at[k],
            device_id={"fft": there},
            device_id_type=MESH,
        ).start()


def keep(send_ref, recv_ref, start, count, me):
    for i in range(count):
        recv_ref[me * WIDE + start + i] = send_ref[start + i, :, pl.ds(me * WIDE, WIDE)]


def arrived(recv_ref, recv_sem):
    block = recv_ref.at[pl.ds(0, WIDE)]
    for k in ORDER:
        pltpu.make_async_copy(block, block, recv_sem.at[k]).wait()


def lines(recv_ref, row):
    flat = recv_ref.reshape(NG * 2 * WIDE, NG)
    return [flat[pl.ds(part * WIDE + row, NG, stride=2 * WIDE), :] for part in (0, 1)]


def field_kernel(
    pick_ref, rh_ref, rl_ref, lh_ref, ll_ref, x_ref, s_ref, o_ref,
    send1, recv1, send2, recv2, ss1, rs1, ss2, rs2,
):
    me = lax.axis_index("fft")
    barrier = pltpu.get_barrier_semaphore()
    for k in range(1, FFT):
        pl.semaphore_signal(barrier, inc=1, device_id={"fft": lax.rem(me + k, FFT)}, device_id_type=MESH)
    pl.semaphore_wait(barrier, FFT - 1)
    pick = pick_ref[0, 0]

    def forward(i, carry):
        start = 2 * i
        rows = []
        for p in (0, 1):
            chosen = x_ref[pick, start + p]
            rows.append(jnp.concatenate([s_ref[0, start + p] * chosen, s_ref[1, start + p] * chosen], axis=1))
        value = on_right(jnp.concatenate(rows, axis=0), rh_ref[...], rl_ref[...])
        value = stack([[value[p * NG:(p + 1) * NG, :NG], value[p * NG:(p + 1) * NG, NG:]] for p in (0, 1)])
        value = on_left(lh_ref[...], ll_ref[...], value)
        for p in (0, 1):
            for part in (0, 1):
                send1[start + p, part] = value[part * NG:(part + 1) * NG, p * NG:(p + 1) * NG]
        exchange(send1, recv1, start, 2, ss1, rs1, me)
        keep(send1, recv1, start, 2, me)
        return carry

    lax.fori_loop(0, WIDE // 2, forward, 0)
    arrived(recv1, rs1)

    first = lax.broadcasted_iota(jnp.int32, (NG, NG), 0)
    last = lax.broadcasted_iota(jnp.int32, (NG, NG), 1)
    signed = lambda n: jnp.where(n < NG // 2, n, n - NG)
    first, last = signed(first), signed(last)
    plane = first * first + last * last

    def middle(i, carry):
        start = 2 * i
        value = stack([lines(recv1, start + p) for p in (0, 1)])
        value = on_left(lh_ref[...], ll_ref[...], value)
        filters = []
        for p in (0, 1):
            second = me * WIDE + start + p
            second = second - NG * (second // (NG // 2))
            square = plane + second * second
            ratio = SCALE / jnp.maximum(square, 1).astype(jnp.float32)
            filters.append(jnp.where(square > 0, ratio, 0.0))
        filters = jnp.concatenate(filters, axis=1)
        value = jnp.concatenate([value[:NG] * filters, value[NG:] * filters], axis=0)
        value = on_left(rh_ref[...], rl_ref[...], value)
        for p in (0, 1):
            for part in (0, 1):
                send2[start + p, part] = value[part * NG:(part + 1) * NG, p * NG:(p + 1) * NG]
        exchange(send2, recv2, start, 2, ss2, rs2, me)
        keep(send2, recv2, start, 2, me)
        return carry

    lax.fori_loop(0, WIDE // 2, middle, 0)
    arrived(recv2, rs2)

    def backward(i, carry):
        start = 2 * i
        value = stack([lines(recv2, start + p) for p in (0, 1)])
        value = on_left(rh_ref[...], rl_ref[...], value)
        value = on_right(unstack(value), lh_ref[...], ll_ref[...])
        for p in (0, 1):
            part = value[p * NG:(p + 1) * NG]
            o_ref[start + p] = part[:, :NG] * s_ref[0, start + p] + part[:, NG:] * s_ref[1, start + p]
        return carry

    lax.fori_loop(0, WIDE // 2, backward, 0)
    for sem, ref in ((ss1, recv1), (ss2, recv2)):
        arrived(ref, sem)


def field(pick, orbitals, sent):
    vmem = pl.BlockSpec(memory_space=pltpu.VMEM)
    dma = pltpu.SemaphoreType.DMA
    consts = [jnp.asarray(t) for t in tables()]
    return pl.pallas_call(
        field_kernel,
        out_shape=jax.ShapeDtypeStruct(orbitals.shape[1:], orbitals.dtype),
        in_specs=[pl.BlockSpec(memory_space=pltpu.SMEM)] + [vmem] * 6,
        out_specs=vmem,
        scratch_shapes=[
            pltpu.VMEM((WIDE, 2, NG, NG), jnp.float32),
            pltpu.VMEM((NG, 2, WIDE, NG), jnp.float32),
            pltpu.VMEM((WIDE, 2, NG, NG), jnp.float32),
            pltpu.VMEM((NG, 2, WIDE, NG), jnp.float32),
            dma((FFT,)), dma((FFT,)), dma((FFT,)), dma((FFT,)),
        ],
        compiler_params=pltpu.CompilerParams(collective_id=0, has_side_effects=True, vmem_limit_bytes=48 << 20),
        name="field",
    )(pick, *consts, orbitals, sent)


def on_device(orbitals, owners, local_pick):
    sent = lax.switch(owners[0], [functools.partial(spread, owner) for owner in range(32)], orbitals)
    return field(local_pick, orbitals, sent)[None]


def solution(mesh):
    in_specs = (P("band", "fft", None, None), P(), P("band", None))
    out_specs = P("band", "fft", None, None)
    return jax.shard_map(on_device, mesh=mesh, in_specs=in_specs, out_specs=out_specs, check_vma=False)
```

```python
import functools
import math

import jax
import jax.numpy as jnp
import numpy as np
from jax import lax
from jax.experimental import pallas as pl
from jax.experimental.pallas import tpu as pltpu
from jax.sharding import PartitionSpec as P

NG = 128
NZ = 8
NX = 4
FFT = 8
WIDE = NG // FFT
MESH = pl.DeviceIdType.MESH
SCALE = 0.25 * NG * math.sqrt(NG) / (NG * NG * NG)


def tables():
    index = np.arange(NG)
    angle = (index[:, None] * index[None, :] % NG) * (2.0 * np.pi / NG)
    high = np.stack([np.cos(angle), np.sin(angle)]).astype(jnp.bfloat16)
    low = (np.stack([np.cos(angle), np.sin(angle)]) - high.astype(np.float64)).astype(jnp.bfloat16)
    return np.stack([high, low])


def split(value):
    high = value.astype(jnp.bfloat16)
    low = (value - high.astype(jnp.float32)).astype(jnp.bfloat16)
    return high, low


def dot(a, b):
    return jnp.dot(a, b, preferred_element_type=jnp.float32)


def on_right(value, high, low):
    vh, vl = split(value)
    return dot(vh, high) + (dot(vl, high) + dot(vh, low))


def on_left(high, low, value):
    vh, vl = split(value)
    return dot(high, vh) + (dot(high, vl) + dot(low, vh))


def stack(parts):
    return jnp.concatenate([jnp.concatenate(p, axis=0) for p in parts], axis=1)


def unstack(value):
    return jnp.concatenate(
        [
            jnp.concatenate([value[:NG, s], value[NG:, s]], axis=1)
            for s in (slice(0, NG), slice(NG, 2 * NG))
        ],
        axis=0,
    )


HALF = NG // 2
SIDE = WIDE // 2
PAIRS = WIDE // 2


def each_shift(body):
    def step(i, carry):
        body(lax.rem(3 * i, FFT))
        return carry

    lax.fori_loop(1, FFT, step, 0)


def exchange(send_ref, recv_ref, start, count, half, send_sem, recv_sem, me):
    high, low = me // NX, lax.rem(me, NX)

    def body(k):
        there = lax.rem(high + k // NX, 2) * NX + lax.rem(low + k, NX)
        pltpu.make_async_remote_copy(
            send_ref.at[pl.ds(start, count), :, pl.ds(there * WIDE + half * SIDE, SIDE)],
            recv_ref.at[pl.ds(me * WIDE + start, count), :, pl.ds(half * SIDE, SIDE)],
            send_sem,
            recv_sem.at[half],
            device_id={"fft": there},
            device_id_type=MESH,
        ).start()

    each_shift(body)


def keep(send_ref, recv_ref, start, me):
    for p in (0, 1):
        recv_ref[me * WIDE + start + p] = send_ref[start + p, :, pl.ds(me * WIDE, WIDE)]


def arrived(recv_ref, half, sem):
    block = recv_ref.at[pl.ds(0, NG - WIDE), :, pl.ds(half * SIDE, SIDE)]
    pltpu.make_async_copy(block, block, sem.at[half]).wait()


def left(recv_ref, sem):
    block = recv_ref.at[pl.ds(0, NG - WIDE)]
    pltpu.make_async_copy(block, block, sem).wait()


def lines(recv_ref, row):
    flat = recv_ref.reshape(NG * 2 * WIDE, NG)
    return [flat[pl.ds(part * WIDE + row, NG, stride=2 * WIDE), :] for part in (0, 1)]


def field_kernel(
    root, pick_ref, core_ref, table_ref, x_ref, o_ref,
    r_ref, l_ref, s_ref, cand, send1, recv1, send2, recv2,
    ring_recv, pair_recv, cand_recv, ring_send, own_send, ss1, rs1, ss2, rs2,
):
    y0, z0 = root // NZ, root % NZ
    me = lax.axis_index("fft")
    band = lax.axis_index("band")
    y, z, c = band // 16, lax.rem(band // 2, NZ), lax.rem(band, 2)
    up, down = lax.rem(z + 1, NZ), lax.rem(z + NZ - 1, NZ)

    def at(yy, zz, cc):
        return {"band": yy * 16 + zz * 2 + cc}

    barrier = pltpu.get_barrier_semaphore()
    greet = [at(y, up, c), at(y, down, c), at(1 - y, z, c), at(y, z, 1 - c)]
    for device in greet:
        pl.semaphore_signal(barrier, inc=1, device_id=device, device_id_type=MESH)

    def greets(k):
        there = {"fft": lax.rem(me + k, FFT)}
        pl.semaphore_signal(barrier, inc=1, device_id=there, device_id_type=MESH)

    each_shift(greets)
    pl.semaphore_wait(barrier, len(greet) + FFT - 1)

    ahead = lax.rem(z - z0 + NZ, NZ)
    home = y == y0
    at_root = jnp.logical_and(home, ahead == 0)
    def remote(src, dst, send_sem, recv_sem, device):
        return pltpu.make_async_remote_copy(
            src, dst, send_sem, recv_sem, device_id=device, device_id_type=MESH
        )

    def waits(ref, sem):
        pltpu.make_async_copy(ref, ref, sem).wait()

    def pass_on(i, source=False):
        entry = jnp.where(i < 2, 1, jnp.where(i < 4, NZ - 1, 0))
        away = jnp.where(home, ahead, lax.rem(ahead - entry + NZ, NZ))
        goes = (
            (away < 4, at(y, up, c)),
            (jnp.logical_or(away == 0, away > 5), at(y, down, c)),
            (jnp.logical_and(home, ahead == entry), at(1 - y, z, c)),
        )
        if source:
            both = cand.at[pl.ds(2 * i, 2)]
            waits(both, cand_recv.at[i])
        for p in (0, 1):
            plane = 2 * i + p
            if source:
                s_ref[c, plane] = jnp.where(core_ref[0] == c, x_ref[c, plane], cand[plane])
            for half in (0, 1):
                here = s_ref.at[c, plane, pl.ds(half * HALF, HALF)]
                sem = ring_recv.at[2 * plane + half]
                if not source:
                    waits(here, sem)
                for way, (condition, device) in enumerate(goes):

                    @pl.when(condition)
                    def _():
                        remote(here, here, ring_send.at[way], sem, device).start()

        here = s_ref.at[c, pl.ds(2 * i, 2)]
        remote(here, here, own_send.at[0], pair_recv.at[i], at(y, z, 1 - c)).start()

    @pl.when(at_root)
    def _():
        def give(i, carry):
            both = pl.ds(2 * i, 2)
            remote(x_ref.at[1 - c, both], cand.at[both], own_send.at[1], cand_recv.at[i], at(y, z, 1 - c)).start()
            return carry

        lax.fori_loop(0, PAIRS, give, 0)

        def source(i, carry):
            pass_on(i, True)
            return carry

        lax.fori_loop(0, PAIRS, source, 0)

    def fill(n, carry):
        cosine, sine = table_ref[n, 0], table_ref[n, 1]
        for ref, near, far in ((r_ref, sine, -sine), (l_ref, -sine, sine)):
            ref[n, :NG, :NG] = cosine
            ref[n, NG:, NG:] = cosine
            ref[n, NG:, :NG] = near
            ref[n, :NG, NG:] = far
        return carry

    lax.fori_loop(0, 2, fill, 0)

    @pl.when(at_root)
    def _():
        crossed = s_ref.at[0, pl.ds(0, 8)]
        waits(crossed, ring_send.at[2])

    pick = pick_ref[0, 0]

    def forward(i):
        start = 2 * i
        rows = []
        waits(s_ref.at[0, pl.ds(0, 2)], pair_recv.at[i])
        for p in (0, 1):
            chosen = x_ref[pick, start + p]
            rows.append(jnp.concatenate([s_ref[0, start + p] * chosen, s_ref[1, start + p] * chosen], axis=1))
        value = on_right(jnp.concatenate(rows, axis=0), r_ref[0], r_ref[1])
        value = stack([[value[p * NG:(p + 1) * NG, :NG], value[p * NG:(p + 1) * NG, NG:]] for p in (0, 1)])
        value = on_left(l_ref[0], l_ref[1], value)
        for p in (0, 1):
            for part in (0, 1):
                send1[start + p, part] = value[part * NG:(part + 1) * NG, p * NG:(p + 1) * NG]
        for half in (0, 1):
            exchange(send1, recv1, start, 2, half, ss1, rs1, me)
        keep(send1, recv1, start, me)

    lag = jnp.where(jnp.logical_and(home, ahead == 1), 3, jnp.where(jnp.logical_and(home, ahead == NZ - 1), 4, 1))

    def stream(i, carry):
        @pl.when(jnp.logical_and(i < PAIRS, jnp.logical_not(at_root)))
        def _():
            pass_on(i)

        @pl.when(jnp.logical_and(i >= lag, i < lag + PAIRS))
        def _():
            forward(i - lag)

        return carry

    lax.fori_loop(0, PAIRS + 4, stream, 0)

    first = lax.broadcasted_iota(jnp.int32, (NG, NG), 0)
    last = lax.broadcasted_iota(jnp.int32, (NG, NG), 1)
    signed = lambda n: jnp.where(n < NG // 2, n, n - NG)
    first, last = signed(first), signed(last)
    flat = first * first + last * last

    def middle(i, carry):
        for half in (0, 1):

            @pl.when(i == half * (PAIRS // 2))
            def _():
                arrived(recv1, half, rs1)

        start = 2 * i
        value = stack([lines(recv1, start + p) for p in (0, 1)])
        value = on_left(l_ref[0], l_ref[1], value)
        filters = []
        for p in (0, 1):
            second = me * WIDE + start + p
            second = second - NG * (second // (NG // 2))
            square = flat + second * second
            ratio = SCALE / jnp.maximum(square, 1).astype(jnp.float32)
            filters.append(jnp.where(square > 0, ratio, 0.0))
        filters = jnp.concatenate(filters, axis=1)
        value = jnp.concatenate([value[:NG] * filters, value[NG:] * filters], axis=0)
        value = on_left(r_ref[0], r_ref[1], value)
        for p in (0, 1):
            for part in (0, 1):
                send2[start + p, part] = value[part * NG:(part + 1) * NG, p * NG:(p + 1) * NG]
        exchange(send2, recv2, start, 2, 0, ss2, rs2, me)
        keep(send2, recv2, start, me)
        return carry

    lax.fori_loop(0, PAIRS, middle, 0)
    exchange(send2, recv2, 0, WIDE, 1, ss2, rs2, me)

    def backward(i, carry):
        for half in (0, 1):

            @pl.when(i == half * (PAIRS // 2))
            def _():
                arrived(recv2, half, rs2)

        start = 2 * i
        value = stack([lines(recv2, start + p) for p in (0, 1)])
        value = on_left(r_ref[0], r_ref[1], value)
        value = on_right(unstack(value), l_ref[0], l_ref[1])
        for p in (0, 1):
            part = value[p * NG:(p + 1) * NG]
            o_ref[start + p] = part[:, :NG] * s_ref[0, start + p] + part[:, NG:] * s_ref[1, start + p]
        return carry

    lax.fori_loop(0, PAIRS, backward, 0)

    whole, half_of, quarter = s_ref.at[0], s_ref.at[0, pl.ds(0, 8)], s_ref.at[0, pl.ds(0, 4)]
    for way in (0, 1):
        for first_entry, block in ((0, half_of), (1, quarter), (NZ - 1, quarter)):
            away = jnp.where(home, ahead, lax.rem(ahead - first_entry + NZ, NZ))
            went = away < 4 if way == 0 else jnp.logical_or(away == 0, away > 5)

            @pl.when(went)
            def _():
                waits(block, ring_send.at[way])

    @pl.when(jnp.logical_and(home, jnp.logical_or(ahead == 1, ahead == NZ - 1)))
    def _():
        waits(quarter, ring_send.at[2])

    waits(whole, own_send.at[0])

    @pl.when(at_root)
    def _():
        waits(whole, own_send.at[1])

    left(recv1, ss1)
    left(recv2, ss2)


def field(root, pick, core, orbitals, table):
    vmem = pl.BlockSpec(memory_space=pltpu.VMEM)
    smem = pl.BlockSpec(memory_space=pltpu.SMEM)
    dma = pltpu.SemaphoreType.DMA
    shapes = [(2, WIDE, NG, NG), (WIDE, NG, NG)]
    shapes += [(WIDE, 2, NG, NG), (NG, 2, WIDE, NG)] * 2
    sems = [(2 * WIDE,), (PAIRS,), (PAIRS,), (3,), (2,), (), (2,), (), (2,)]
    return pl.pallas_call(
        functools.partial(field_kernel, root),
        out_shape=jax.ShapeDtypeStruct(orbitals.shape[1:], orbitals.dtype),
        in_specs=[smem] * 2 + [vmem] * 2,
        out_specs=vmem,
        scratch_shapes=[pltpu.VMEM((2, 2 * NG, 2 * NG), jnp.bfloat16)] * 2
        + [pltpu.VMEM(shape, jnp.float32) for shape in shapes]
        + [dma(shape) for shape in sems],
        compiler_params=pltpu.CompilerParams(collective_id=root, has_side_effects=True, vmem_limit_bytes=48 << 20),
        name=f"field_{root}",
    )(pick, core, table, orbitals)


def on_device(orbitals, owners, local_pick):
    table = lax.optimization_barrier(jnp.asarray(tables()))
    branches = [functools.partial(field, root) for root in range(2 * NZ)]
    return lax.switch(owners[0] // 2, branches, local_pick, owners % 2, orbitals, table)[None]


def solution(mesh):
    in_specs = (P("band", "fft", None, None), P(), P("band", None))
    out_specs = P("band", "fft", None, None)
    return jax.shard_map(on_device, mesh=mesh, in_specs=in_specs, out_specs=out_specs, check_vma=False)
```

```python
import functools
import math

import jax
import jax.numpy as jnp
import numpy as np
from jax import lax
from jax.experimental import pallas as pl
from jax.experimental.pallas import tpu as pltpu
from jax.sharding import PartitionSpec as P

NG = 128
NZ = 8
NX = 4
FFT = 8
WIDE = NG // FFT
MESH = pl.DeviceIdType.MESH
SCALE = 0.25 * NG * math.sqrt(NG) / (NG * NG * NG)


def tables():
    index = np.arange(NG)
    angle = (index[:, None] * index[None, :] % NG) * (2.0 * np.pi / NG)
    high = np.stack([np.cos(angle), np.sin(angle)]).astype(jnp.bfloat16)
    low = (np.stack([np.cos(angle), np.sin(angle)]) - high.astype(np.float64)).astype(jnp.bfloat16)
    return np.stack([high, low])


def split(value):
    high = value.astype(jnp.bfloat16)
    low = (value - high.astype(jnp.float32)).astype(jnp.bfloat16)
    return high, low


def dot(a, b):
    return jnp.dot(a, b, preferred_element_type=jnp.float32)


def on_right(value, high, low):
    vh, vl = split(value)
    return dot(vh, high) + (dot(vl, high) + dot(vh, low))


def on_left(high, low, value):
    vh, vl = split(value)
    return dot(high, vh) + (dot(high, vl) + dot(low, vh))


def stack(parts):
    return jnp.concatenate([jnp.concatenate(p, axis=0) for p in parts], axis=1)


def unstack(value):
    return jnp.concatenate(
        [
            jnp.concatenate([value[:NG, s], value[NG:, s]], axis=1)
            for s in (slice(0, NG), slice(NG, 2 * NG))
        ],
        axis=0,
    )


HALF = NG // 2
SIDE = WIDE // 2
PAIRS = WIDE // 2


def each_shift(body):
    def step(i, carry):
        body(lax.rem(3 * i, FFT))
        return carry

    lax.fori_loop(1, FFT, step, 0)


def exchange(send_ref, recv_ref, start, count, half, send_sem, recv_sem, me):
    high, low = me // NX, lax.rem(me, NX)

    def body(k):
        there = lax.rem(high + k // NX, 2) * NX + lax.rem(low + k, NX)
        pltpu.make_async_remote_copy(
            send_ref.at[pl.ds(start, count), :, pl.ds(there * WIDE + half * SIDE, SIDE)],
            recv_ref.at[pl.ds(me * WIDE + start, count), :, pl.ds(half * SIDE, SIDE)],
            send_sem,
            recv_sem.at[half],
            device_id={"fft": there},
            device_id_type=MESH,
        ).start()

    each_shift(body)


def keep(send_ref, recv_ref, start, me):
    for p in (0, 1):
        recv_ref[me * WIDE + start + p] = send_ref[start + p, :, pl.ds(me * WIDE, WIDE)]


def arrived(recv_ref, half, sem):
    block = recv_ref.at[pl.ds(0, NG - WIDE), :, pl.ds(half * SIDE, SIDE)]
    pltpu.make_async_copy(block, block, sem.at[half]).wait()


def left(recv_ref, sem):
    block = recv_ref.at[pl.ds(0, NG - WIDE)]
    pltpu.make_async_copy(block, block, sem).wait()


def lines(recv_ref, row):
    flat = recv_ref.reshape(NG * 2 * WIDE, NG)
    return [flat[pl.ds(part * WIDE + row, NG, stride=2 * WIDE), :] for part in (0, 1)]


def field_kernel(
    root, pick_ref, core_ref, table_hbm, x_hbm, o_hbm,
    table_ref, x_ref, o_ref, r_ref, l_ref, s_ref, cand, send1, recv1, send2, recv2,
    ring_recv, pair_recv, cand_recv, ring_send, own_send, ss1, rs1, ss2, rs2, own_copy,
):
    y0, z0 = root // NZ, root % NZ
    me = lax.axis_index("fft")
    band = lax.axis_index("band")
    y, z, c = band // 16, lax.rem(band // 2, NZ), lax.rem(band, 2)
    up, down = lax.rem(z + 1, NZ), lax.rem(z + NZ - 1, NZ)

    def at(yy, zz, cc):
        return {"band": yy * 16 + zz * 2 + cc}

    x_copy = pltpu.make_async_copy(x_hbm, x_ref, own_copy.at[0])
    table_copy = pltpu.make_async_copy(table_hbm, table_ref, own_copy.at[1])
    x_copy.start()
    table_copy.start()
    barrier = pltpu.get_barrier_semaphore()
    greet = [at(y, up, c), at(y, down, c), at(1 - y, z, c), at(y, z, 1 - c)]
    for device in greet:
        pl.semaphore_signal(barrier, inc=1, device_id=device, device_id_type=MESH)

    def greets(k):
        there = {"fft": lax.rem(me + k, FFT)}
        pl.semaphore_signal(barrier, inc=1, device_id=there, device_id_type=MESH)

    each_shift(greets)
    x_copy.wait()
    pl.semaphore_wait(barrier, len(greet) + FFT - 1)

    ahead = lax.rem(z - z0 + NZ, NZ)
    home = y == y0
    at_root = jnp.logical_and(home, ahead == 0)
    def remote(src, dst, send_sem, recv_sem, device):
        return pltpu.make_async_remote_copy(
            src, dst, send_sem, recv_sem, device_id=device, device_id_type=MESH
        )

    def waits(ref, sem):
        pltpu.make_async_copy(ref, ref, sem).wait()

    def ship(pair, q, way):
        here = s_ref.at[c, 2 * pair + q // 2, pl.ds(lax.rem(q, 2) * HALF, HALF)]
        ring = y * 16 + jnp.where(way == 0, up, down) * 2 + c
        device = {"band": jnp.where(way == 2, (1 - y) * 16 + z * 2 + c, ring)}
        remote(here, here, ring_send.at[way], ring_recv.at[4 * pair + q], device).start()

    def share(pair):
        here = s_ref.at[c, pl.ds(2 * pair, 2)]
        remote(here, here, own_send.at[0], pair_recv.at[pair], at(y, z, 1 - c)).start()

    def repeat(start, stop, body):
        def step(i, carry):
            body(i)
            return carry

        lax.fori_loop(start, stop, step, 0)

    def pass_on(pair):
        entry = jnp.where(pair < 2, 1, jnp.where(pair < 4, NZ - 1, 0))
        away = jnp.where(home, ahead, lax.rem(ahead - entry + NZ, NZ))
        goes = (
            away < 4,
            jnp.logical_or(away == 0, away > 5),
            jnp.logical_and(home, ahead == entry),
        )

        def quarter(q):
            here = s_ref.at[c, 2 * pair + q // 2, pl.ds(lax.rem(q, 2) * HALF, HALF)]
            waits(here, ring_recv.at[4 * pair + q])
            for way, condition in enumerate(goes):

                @pl.when(condition)
                def _():
                    ship(pair, q, way)

        repeat(0, 4, quarter)
        share(pair)

    def turned(i):
        return jnp.where(i < 4, lax.rem(i + 2, 4), i)

    def order(i):
        near = jnp.where(ahead > 4, turned(i), i)
        k = lax.rem(i + 4, PAIRS)
        far = jnp.where(ahead > 4, turned(k), k)
        swapped = jnp.logical_and(ahead == 0, jnp.logical_or(k == 1, k == 2))
        return jnp.where(home, near, jnp.where(swapped, 3 - k, far))

    @pl.when(at_root)
    def _():
        def nth(j):
            return jnp.where(j < 6, 2 * lax.rem(j, 3) + j // 3, j)

        def give(j):
            both = pl.ds(2 * nth(j), 2)
            remote(x_ref.at[1 - c, both], cand.at[both], own_send.at[1], cand_recv.at[nth(j)], at(y, z, 1 - c)).start()

        repeat(0, PAIRS, give)

        def source(j):
            pair = nth(j)
            waits(cand.at[pl.ds(0, 2)], cand_recv.at[pair])
            for p in (0, 1):
                plane = 2 * pair + p
                s_ref[c, plane] = jnp.where(core_ref[0] == c, x_ref[c, plane], cand[plane])
            repeat(0, 4, lambda q: ship(pair, q, jnp.where(j < 6, lax.rem(j, 3), 2)))
            share(pair)

        repeat(0, PAIRS, source)

        def rest(i):
            repeat(0, 8, lambda q: ship(jnp.where(q < 4, i, turned(i)), lax.rem(q, 4), q // 4))

        repeat(2, PAIRS, rest)

    table_copy.wait()

    def fill(n, carry):
        cosine, sine = table_ref[n, 0], table_ref[n, 1]
        for ref, near, far in ((r_ref, sine, -sine), (l_ref, -sine, sine)):
            ref[n, :NG, :NG] = cosine
            ref[n, NG:, NG:] = cosine
            ref[n, NG:, :NG] = near
            ref[n, :NG, NG:] = far
        return carry

    lax.fori_loop(0, 2, fill, 0)

    @pl.when(at_root)
    def _():
        crossed = s_ref.at[0, pl.ds(0, 8)]
        waits(crossed, ring_send.at[2])

    pick = pick_ref[0, 0]

    def forward(i):
        pair = order(i)
        start = 2 * pair
        rows = []
        waits(s_ref.at[0, pl.ds(0, 2)], pair_recv.at[pair])
        for p in (0, 1):
            chosen = x_ref[pick, start + p]
            rows.append(jnp.concatenate([s_ref[0, start + p] * chosen, s_ref[1, start + p] * chosen], axis=1))
        value = on_right(jnp.concatenate(rows, axis=0), r_ref[0], r_ref[1])
        value = stack([[value[p * NG:(p + 1) * NG, :NG], value[p * NG:(p + 1) * NG, NG:]] for p in (0, 1)])
        value = on_left(l_ref[0], l_ref[1], value)
        for p in (0, 1):
            for part in (0, 1):
                send1[start + p, part] = value[part * NG:(part + 1) * NG, p * NG:(p + 1) * NG]
        for half in (0, 1):
            exchange(send1, recv1, start, 2, half, ss1, rs1, me)
        keep(send1, recv1, start, me)

    lag = jnp.where(jnp.logical_and(home, jnp.logical_or(ahead == 1, ahead == NZ - 1)), 3, 1)

    def stream(i, carry):
        @pl.when(jnp.logical_and(i < PAIRS, jnp.logical_not(at_root)))
        def _():
            pass_on(order(i))

        @pl.when(jnp.logical_and(i >= lag, i < lag + PAIRS))
        def _():
            forward(i - lag)

        return carry

    lax.fori_loop(0, PAIRS + 3, stream, 0)

    first = lax.broadcasted_iota(jnp.int32, (NG, NG), 0)
    last = lax.broadcasted_iota(jnp.int32, (NG, NG), 1)
    signed = lambda n: jnp.where(n < NG // 2, n, n - NG)
    first, last = signed(first), signed(last)
    flat = first * first + last * last

    def middle(i, carry):
        for half in (0, 1):

            @pl.when(i == half * (PAIRS // 2))
            def _():
                arrived(recv1, half, rs1)

        start = 2 * i
        value = stack([lines(recv1, start + p) for p in (0, 1)])
        value = on_left(l_ref[0], l_ref[1], value)
        filters = []
        for p in (0, 1):
            second = me * WIDE + start + p
            second = second - NG * (second // (NG // 2))
            square = flat + second * second
            ratio = SCALE / jnp.maximum(square, 1).astype(jnp.float32)
            filters.append(jnp.where(square > 0, ratio, 0.0))
        filters = jnp.concatenate(filters, axis=1)
        value = jnp.concatenate([value[:NG] * filters, value[NG:] * filters], axis=0)
        value = on_left(r_ref[0], r_ref[1], value)
        for p in (0, 1):
            for part in (0, 1):
                send2[start + p, part] = value[part * NG:(part + 1) * NG, p * NG:(p + 1) * NG]
        exchange(send2, recv2, start, 2, 0, ss2, rs2, me)
        keep(send2, recv2, start, me)
        return carry

    lax.fori_loop(0, PAIRS, middle, 0)
    exchange(send2, recv2, 0, WIDE, 1, ss2, rs2, me)

    def backward(i, carry):
        for half in (0, 1):

            @pl.when(i == half * (PAIRS // 2))
            def _():
                arrived(recv2, half, rs2)

        start = 2 * i
        value = stack([lines(recv2, start + p) for p in (0, 1)])
        value = on_left(r_ref[0], r_ref[1], value)
        value = on_right(unstack(value), l_ref[0], l_ref[1])
        for p in (0, 1):
            part = value[p * NG:(p + 1) * NG]
            o_ref[start + p] = part[:, :NG] * s_ref[0, start + p] + part[:, NG:] * s_ref[1, start + p]
        both = pl.ds(start, 2)
        pltpu.make_async_copy(o_ref.at[both], o_hbm.at[both], own_copy.at[2]).start()
        return carry

    lax.fori_loop(0, PAIRS, backward, 0)

    whole, half_of, quarter = s_ref.at[0], s_ref.at[0, pl.ds(0, 8)], s_ref.at[0, pl.ds(0, 4)]
    for way in (0, 1):
        for first_entry, block in ((0, half_of), (1, quarter), (NZ - 1, quarter)):
            away = jnp.where(home, ahead, lax.rem(ahead - first_entry + NZ, NZ))
            went = away < 4 if way == 0 else jnp.logical_or(away == 0, away > 5)

            @pl.when(went)
            def _():
                waits(block, ring_send.at[way])

    @pl.when(jnp.logical_and(home, jnp.logical_or(ahead == 1, ahead == NZ - 1)))
    def _():
        waits(quarter, ring_send.at[2])

    waits(whole, own_send.at[0])

    @pl.when(at_root)
    def _():
        waits(whole, own_send.at[1])

    pltpu.make_async_copy(o_ref, o_hbm, own_copy.at[2]).wait()
    left(recv1, ss1)
    left(recv2, ss2)


def field(root, pick, core, orbitals, table):
    smem = pl.BlockSpec(memory_space=pltpu.SMEM)
    place = pl.BlockSpec(memory_space=pl.ANY)
    dma = pltpu.SemaphoreType.DMA
    shapes = [(2, WIDE, NG, NG), (WIDE, NG, NG)]
    shapes += [(WIDE, 2, NG, NG), (NG, 2, WIDE, NG)] * 2
    sems = [(2 * WIDE,), (PAIRS,), (PAIRS,), (3,), (2,), (), (2,), (), (2,), (3,)]
    return pl.pallas_call(
        functools.partial(field_kernel, root),
        out_shape=jax.ShapeDtypeStruct(orbitals.shape[1:], orbitals.dtype),
        in_specs=[smem] * 2 + [place] * 2,
        out_specs=place,
        scratch_shapes=[pltpu.VMEM(table.shape, table.dtype), pltpu.VMEM(orbitals.shape, jnp.float32), pltpu.VMEM(orbitals.shape[1:], jnp.float32)]
        + [pltpu.VMEM((2, 2 * NG, 2 * NG), jnp.bfloat16)] * 2
        + [pltpu.VMEM(shape, jnp.float32) for shape in shapes]
        + [dma(shape) for shape in sems],
        compiler_params=pltpu.CompilerParams(collective_id=root, has_side_effects=True, vmem_limit_bytes=48 << 20),
        name=f"field_{root}",
    )(pick, core, table, orbitals)


def on_device(orbitals, owners, local_pick):
    table = lax.optimization_barrier(jnp.asarray(tables()))
    branches = [functools.partial(field, root) for root in range(2 * NZ)]
    return lax.switch(owners[0] // 2, branches, local_pick, owners % 2, orbitals, table)[None]


def solution(mesh):
    in_specs = (P("band", "fft", None, None), P(), P("band", None))
    out_specs = P("band", "fft", None, None)
    return jax.shard_map(on_device, mesh=mesh, in_specs=in_specs, out_specs=out_specs, check_vma=False)
```

```python
import functools
import math

import jax
import jax.numpy as jnp
import numpy as np
from jax import lax
from jax.experimental import pallas as pl
from jax.experimental.pallas import tpu as pltpu
from jax.sharding import PartitionSpec as P

NG = 128
NZ = 8
NX = 4
FFT = 8
WIDE = NG // FFT
MESH = pl.DeviceIdType.MESH
SCALE = 0.25 * NG * math.sqrt(NG) / (NG * NG * NG)


def tables():
    index = np.arange(NG)
    angle = (index[:, None] * index[None, :] % NG) * (2.0 * np.pi / NG)
    high = np.stack([np.cos(angle), np.sin(angle)]).astype(jnp.bfloat16)
    low = (np.stack([np.cos(angle), np.sin(angle)]) - high.astype(np.float64)).astype(jnp.bfloat16)
    return np.stack([high, low])


def split(value):
    high = value.astype(jnp.bfloat16)
    low = (value - high.astype(jnp.float32)).astype(jnp.bfloat16)
    return high, low


def dot(a, b):
    return jnp.dot(a, b, preferred_element_type=jnp.float32)


def on_right(value, high, low):
    vh, vl = split(value)
    return dot(vh, high) + (dot(vl, high) + dot(vh, low))


def on_left(high, low, value):
    vh, vl = split(value)
    return dot(high, vh) + (dot(high, vl) + dot(low, vh))


def stack(parts):
    return jnp.concatenate([jnp.concatenate(p, axis=0) for p in parts], axis=1)


def unstack(value):
    return jnp.concatenate(
        [
            jnp.concatenate([value[:NG, s], value[NG:, s]], axis=1)
            for s in (slice(0, NG), slice(NG, 2 * NG))
        ],
        axis=0,
    )


HALF = NG // 2
SIDE = WIDE // 2
PAIRS = WIDE // 2
PROMPT = 6


def each_shift(body):
    def step(i, carry):
        body(lax.rem(3 * i, FFT))
        return carry

    lax.fori_loop(1, FFT, step, 0)


def exchange(send_ref, recv_ref, start, count, half, send_sem, recv_sem, me):
    high, low = me // NX, lax.rem(me, NX)

    def body(k):
        there = lax.rem(high + k // NX, 2) * NX + lax.rem(low + k, NX)
        pltpu.make_async_remote_copy(
            send_ref.at[pl.ds(start, count), :, pl.ds(there * WIDE + half * SIDE, SIDE)],
            recv_ref.at[pl.ds(me * WIDE + start, count), :, pl.ds(half * SIDE, SIDE)],
            send_sem,
            recv_sem.at[half],
            device_id={"fft": there},
            device_id_type=MESH,
        ).start()

    each_shift(body)


def keep(send_ref, recv_ref, start, me):
    for p in (0, 1):
        recv_ref[me * WIDE + start + p] = send_ref[start + p, :, pl.ds(me * WIDE, WIDE)]


def arrived(recv_ref, half, sem):
    block = recv_ref.at[pl.ds(0, NG - WIDE), :, pl.ds(half * SIDE, SIDE)]
    pltpu.make_async_copy(block, block, sem.at[half]).wait()


def left(recv_ref, sem):
    block = recv_ref.at[pl.ds(0, NG - WIDE)]
    pltpu.make_async_copy(block, block, sem).wait()


def lines(recv_ref, row):
    flat = recv_ref.reshape(NG * 2 * WIDE, NG)
    return [flat[pl.ds(part * WIDE + row, NG, stride=2 * WIDE), :] for part in (0, 1)]


def field_kernel(
    root, pick_ref, core_ref, table_hbm, x_hbm, o_hbm,
    table_ref, x_ref, o_ref, r_ref, l_ref, s_ref, cand, send1, recv1, send2, recv2,
    ring_recv, pair_recv, cand_recv, ring_send, own_send, ss1, rs1, ss2, rs2, own_copy,
):
    y0, z0 = root // NZ, root % NZ
    me = lax.axis_index("fft")
    band = lax.axis_index("band")
    y, z, c = band // 16, lax.rem(band // 2, NZ), lax.rem(band, 2)
    up, down = lax.rem(z + 1, NZ), lax.rem(z + NZ - 1, NZ)

    def at(yy, zz, cc):
        return {"band": yy * 16 + zz * 2 + cc}

    x_copy = pltpu.make_async_copy(x_hbm, x_ref, own_copy.at[0])
    table_copy = pltpu.make_async_copy(table_hbm, table_ref, own_copy.at[1])
    x_copy.start()
    table_copy.start()
    barrier = pltpu.get_barrier_semaphore()
    greet = [at(y, up, c), at(y, down, c), at(1 - y, z, c), at(y, z, 1 - c)]
    for device in greet:
        pl.semaphore_signal(barrier, inc=1, device_id=device, device_id_type=MESH)

    def greets(k):
        there = {"fft": lax.rem(me + k, FFT)}
        pl.semaphore_signal(barrier, inc=1, device_id=there, device_id_type=MESH)

    each_shift(greets)
    x_copy.wait()
    pl.semaphore_wait(barrier, len(greet) + FFT - 1)

    ahead = lax.rem(z - z0 + NZ, NZ)
    home = y == y0
    at_root = jnp.logical_and(home, ahead == 0)
    def remote(src, dst, send_sem, recv_sem, device):
        return pltpu.make_async_remote_copy(
            src, dst, send_sem, recv_sem, device_id=device, device_id_type=MESH
        )

    def waits(ref, sem):
        pltpu.make_async_copy(ref, ref, sem).wait()

    def ship(pair, q, way):
        here = s_ref.at[c, 2 * pair + q // 2, pl.ds(lax.rem(q, 2) * HALF, HALF)]
        ring = y * 16 + jnp.where(way == 0, up, down) * 2 + c
        device = {"band": jnp.where(way == 2, (1 - y) * 16 + z * 2 + c, ring)}
        remote(here, here, ring_send.at[way], ring_recv.at[4 * pair + q], device).start()

    def share(pair):
        here = s_ref.at[c, pl.ds(2 * pair, 2)]
        remote(here, here, own_send.at[0], pair_recv.at[pair], at(y, z, 1 - c)).start()

    def repeat(start, stop, body):
        def step(i, carry):
            body(i)
            return carry

        lax.fori_loop(start, stop, step, 0)

    def pass_on(pair):
        entry = jnp.where(pair < 2, 1, jnp.where(pair < 4, NZ - 1, 0))
        away = jnp.where(home, ahead, lax.rem(ahead - entry + NZ, NZ))
        goes = (
            away < 4,
            jnp.logical_or(away == 0, away > 5),
            jnp.logical_and(home, ahead == entry),
        )

        def quarter(q):
            here = s_ref.at[c, 2 * pair + q // 2, pl.ds(lax.rem(q, 2) * HALF, HALF)]
            waits(here, ring_recv.at[4 * pair + q])
            for way, condition in enumerate(goes):

                @pl.when(condition)
                def _():
                    ship(pair, q, way)

        repeat(0, 4, quarter)
        share(pair)

    def turned(i):
        return jnp.where(i < 4, lax.rem(i + 2, 4), i)

    def order(i):
        near = jnp.where(ahead > 4, turned(i), i)
        k = lax.rem(i + 4, PAIRS)
        far = jnp.where(ahead > 4, turned(k), k)
        swapped = jnp.logical_and(ahead == 0, jnp.logical_or(k == 1, k == 2))
        return jnp.where(home, near, jnp.where(swapped, 3 - k, far))

    @pl.when(at_root)
    def _():
        def nth(j):
            return jnp.where(j < 6, 2 * lax.rem(j, 3) + j // 3, j)

        def give(j):
            both = pl.ds(2 * nth(j), 2)
            remote(x_ref.at[1 - c, both], cand.at[both], own_send.at[1], cand_recv.at[nth(j)], at(y, z, 1 - c)).start()

        repeat(0, PAIRS, give)

        def source(j):
            pair = nth(j)
            waits(cand.at[pl.ds(0, 2)], cand_recv.at[pair])
            for p in (0, 1):
                plane = 2 * pair + p
                s_ref[c, plane] = jnp.where(core_ref[0] == c, x_ref[c, plane], cand[plane])
            repeat(0, 4, lambda q: ship(pair, q, jnp.where(j < 6, lax.rem(j, 3), 2)))
            share(pair)

        repeat(0, PAIRS, source)

        def rest(i):
            repeat(0, 8, lambda q: ship(jnp.where(q < 4, i, turned(i)), lax.rem(q, 4), q // 4))

        repeat(2, PAIRS, rest)

    table_copy.wait()

    def fill(n, carry):
        cosine, sine = table_ref[n, 0], table_ref[n, 1]
        for ref, near, far in ((r_ref, sine, -sine), (l_ref, -sine, sine)):
            ref[n, :NG, :NG] = cosine
            ref[n, NG:, NG:] = cosine
            ref[n, NG:, :NG] = near
            ref[n, :NG, NG:] = far
        return carry

    lax.fori_loop(0, 2, fill, 0)

    @pl.when(at_root)
    def _():
        crossed = s_ref.at[0, pl.ds(0, 8)]
        waits(crossed, ring_send.at[2])

    pick = pick_ref[0, 0]

    def forward(i):
        pair = order(i)
        start = 2 * pair
        rows = []
        waits(s_ref.at[0, pl.ds(0, 2)], pair_recv.at[pair])
        for p in (0, 1):
            chosen = x_ref[pick, start + p]
            rows.append(jnp.concatenate([s_ref[0, start + p] * chosen, s_ref[1, start + p] * chosen], axis=1))
        value = on_right(jnp.concatenate(rows, axis=0), r_ref[0], r_ref[1])
        value = stack([[value[p * NG:(p + 1) * NG, :NG], value[p * NG:(p + 1) * NG, NG:]] for p in (0, 1)])
        value = on_left(l_ref[0], l_ref[1], value)
        for p in (0, 1):
            for part in (0, 1):
                send1[start + p, part] = value[part * NG:(part + 1) * NG, p * NG:(p + 1) * NG]
        exchange(send1, recv1, start, 2, 0, ss1, rs1, me)

        @pl.when(i < PROMPT)
        def _():
            exchange(send1, recv1, start, 2, 1, ss1, rs1, me)

        keep(send1, recv1, start, me)

    lag = jnp.where(jnp.logical_and(home, jnp.logical_or(ahead == 1, ahead == NZ - 1)), 3, 1)

    def stream(i, carry):
        @pl.when(jnp.logical_and(i < PAIRS, jnp.logical_not(at_root)))
        def _():
            pass_on(order(i))

        @pl.when(jnp.logical_and(i >= lag, i < lag + PAIRS))
        def _():
            forward(i - lag)

        return carry

    lax.fori_loop(0, PAIRS + 3, stream, 0)
    repeat(PROMPT, PAIRS, lambda i: exchange(send1, recv1, 2 * order(i), 2, 1, ss1, rs1, me))

    first = lax.broadcasted_iota(jnp.int32, (NG, NG), 0)
    last = lax.broadcasted_iota(jnp.int32, (NG, NG), 1)
    signed = lambda n: jnp.where(n < NG // 2, n, n - NG)
    first, last = signed(first), signed(last)
    flat = first * first + last * last

    def middle(i, carry):
        for half in (0, 1):

            @pl.when(i == half * (PAIRS // 2))
            def _():
                arrived(recv1, half, rs1)

        start = 2 * i
        value = stack([lines(recv1, start + p) for p in (0, 1)])
        value = on_left(l_ref[0], l_ref[1], value)
        filters = []
        for p in (0, 1):
            second = me * WIDE + start + p
            second = second - NG * (second // (NG // 2))
            square = flat + second * second
            ratio = SCALE / jnp.maximum(square, 1).astype(jnp.float32)
            filters.append(jnp.where(square > 0, ratio, 0.0))
        filters = jnp.concatenate(filters, axis=1)
        value = jnp.concatenate([value[:NG] * filters, value[NG:] * filters], axis=0)
        value = on_left(r_ref[0], r_ref[1], value)
        for p in (0, 1):
            for part in (0, 1):
                send2[start + p, part] = value[part * NG:(part + 1) * NG, p * NG:(p + 1) * NG]
        exchange(send2, recv2, start, 2, 0, ss2, rs2, me)
        keep(send2, recv2, start, me)
        return carry

    lax.fori_loop(0, PAIRS, middle, 0)
    exchange(send2, recv2, 0, WIDE, 1, ss2, rs2, me)

    def backward(i, carry):
        for half in (0, 1):

            @pl.when(i == half * (PAIRS // 2))
            def _():
                arrived(recv2, half, rs2)

        start = 2 * i
        value = stack([lines(recv2, start + p) for p in (0, 1)])
        value = on_left(r_ref[0], r_ref[1], value)
        value = on_right(unstack(value), l_ref[0], l_ref[1])
        for p in (0, 1):
            part = value[p * NG:(p + 1) * NG]
            o_ref[start + p] = part[:, :NG] * s_ref[0, start + p] + part[:, NG:] * s_ref[1, start + p]
        both = pl.ds(start, 2)
        pltpu.make_async_copy(o_ref.at[both], o_hbm.at[both], own_copy.at[2]).start()
        return carry

    lax.fori_loop(0, PAIRS, backward, 0)

    whole, half_of, quarter = s_ref.at[0], s_ref.at[0, pl.ds(0, 8)], s_ref.at[0, pl.ds(0, 4)]
    for way in (0, 1):
        for first_entry, block in ((0, half_of), (1, quarter), (NZ - 1, quarter)):
            away = jnp.where(home, ahead, lax.rem(ahead - first_entry + NZ, NZ))
            went = away < 4 if way == 0 else jnp.logical_or(away == 0, away > 5)

            @pl.when(went)
            def _():
                waits(block, ring_send.at[way])

    @pl.when(jnp.logical_and(home, jnp.logical_or(ahead == 1, ahead == NZ - 1)))
    def _():
        waits(quarter, ring_send.at[2])

    waits(whole, own_send.at[0])

    @pl.when(at_root)
    def _():
        waits(whole, own_send.at[1])

    pltpu.make_async_copy(o_ref, o_hbm, own_copy.at[2]).wait()
    left(recv1, ss1)
    left(recv2, ss2)


def field(root, pick, core, orbitals, table):
    smem = pl.BlockSpec(memory_space=pltpu.SMEM)
    place = pl.BlockSpec(memory_space=pl.ANY)
    dma = pltpu.SemaphoreType.DMA
    shapes = [(2, WIDE, NG, NG), (WIDE, NG, NG)]
    shapes += [(WIDE, 2, NG, NG), (NG, 2, WIDE, NG)] * 2
    sems = [(2 * WIDE,), (PAIRS,), (PAIRS,), (3,), (2,), (), (2,), (), (2,), (3,)]
    return pl.pallas_call(
        functools.partial(field_kernel, root),
        out_shape=jax.ShapeDtypeStruct(orbitals.shape[1:], orbitals.dtype),
        in_specs=[smem] * 2 + [place] * 2,
        out_specs=place,
        scratch_shapes=[pltpu.VMEM(table.shape, table.dtype), pltpu.VMEM(orbitals.shape, jnp.float32), pltpu.VMEM(orbitals.shape[1:], jnp.float32)]
        + [pltpu.VMEM((2, 2 * NG, 2 * NG), jnp.bfloat16)] * 2
        + [pltpu.VMEM(shape, jnp.float32) for shape in shapes]
        + [dma(shape) for shape in sems],
        compiler_params=pltpu.CompilerParams(collective_id=root, has_side_effects=True, vmem_limit_bytes=48 << 20),
        name=f"field_{root}",
    )(pick, core, table, orbitals)


def on_device(orbitals, owners, local_pick):
    table = lax.optimization_barrier(jnp.asarray(tables()))
    branches = [functools.partial(field, root) for root in range(2 * NZ)]
    return lax.switch(owners[0] // 2, branches, local_pick, owners % 2, orbitals, table)[None]


def solution(mesh):
    in_specs = (P("band", "fft", None, None), P(), P("band", None))
    out_specs = P("band", "fft", None, None)
    return jax.shard_map(on_device, mesh=mesh, in_specs=in_specs, out_specs=out_specs, check_vma=False)
```
